32 devices in a mesh: gx: 4 (over y, x), gy: 4 (over z), gz: 2 (over core).
Axes of the slice: x: 2, y: 2, z: 4, core: 2. Of those that a mesh axis runs over, the one named last changes fastest.
Arguments:
- state: float32 [16, 32, 64, 256], P('gx', 'gy', 'gz'), may hold values from -6 to 6
- convection: bfloat16 [16, 32, 64, 4096], P('gx', 'gy', 'gz'), may hold values from -0.375 to 0.375
- inverse_mass: bfloat16 [16, 32, 64, 4096], P('gx', 'gy', 'gz'), may hold values from -0.75 to 0.75
- face_coupling: bfloat16 [96, 64], replicated, may hold values from -0.3125 to 0.3125
- lower_bound: float32 [16, 32, 64, 256], P('gx', 'gy', 'gz'), may hold values from -3 to -1
- upper_bound: float32 [16, 32, 64, 256], P('gx', 'gy', 'gz'), may hold values from 1 to 3
- new_owner: int32 [32, 1024, 1], P(('gx', 'gy', 'gz')), may hold values from 0 to 31; in each aligned block of 1024 rows (0 to 1023, 1024 to 2047, ..., all dimensions but the last counted through in order) at most 64 rows name the same one
Outputs:
- handed: float32 [65536, 256], P(('gx', 'gy', 'gz'))
The draws below stay inside these ranges and needn't reach their ends.
Inputs may be any that keep to these rules, and one draw needn't show every extreme that they name: `new_owner`: among the zones of one device no owner is named more than 64 times, a bound that some block reaches.
All inputs are finite; a program needn't handle non-finite values.
Results may differ from the reference program's by a relative error of at most 0.003.
Values may be sent and summed in bfloat16 or wider, within the bound.
A program may use at most 128 MiB of HBM per device.

```python
import math
import jax
import jax.numpy as jnp
import numpy as np
from jax import lax

COMP = 4
DOFS = 64
STEPS = 2
EX = 4
EY = 8
EZ = 32
ZONES_DEV = 1024
CAP = 64
NX = 16
NY = 32
NZ = 64
N_GX = 4
N_GY = 4
N_GZ = 2
DEVICES = 32


def levels(key, extent, split, low, high):
    level = 1.0
    for position, parts in split:
        heights = jax.random.uniform(jax.random.fold_in(jax.random.fold_in(key, 6), position), (parts,), jnp.float32, low / len(split), high / len(split))
        level = level * jnp.repeat(jnp.exp(heights), extent[position] // parts).reshape((-1,) + (1,) * (len(extent) - 1 - position))
    return level


def shared_out(key, own, number, rows, count, top, reach, slope):
    order = jax.random.permutation(key, count)
    heavy_load, common = shares(count, rows * top, reach, slope, True), shares(count, rows * top, reach, slope, False)
    places = jnp.arange(count)

    def named(sizes, turn):
        used = int((sizes > 0).sum())
        fixed = max(1, used // 4)
        moved = fixed + (places - fixed + turn * (used - fixed)) % max(1, count - fixed)
        return jnp.zeros((count,), jnp.int32).at[order[jnp.where(places < fixed, places, moved)]].set(jnp.asarray(sizes, jnp.int32))

    sizes = jnp.where(number % 4 == 0, named(heavy_load, number // 4), named(common, number - number // 4 - 1))
    mixed = jax.random.permutation(jax.random.fold_in(own, 3), count)
    giver, taker = mixed[0:count // 2 * 2:2], mixed[1:count // 2 * 2:2]
    room = jnp.minimum(sizes[giver] - 1, reach - sizes[taker]) // 2
    room = jnp.where((giver == order[0]) | (taker == order[0]) | (sizes[taker] == 0), 0, jnp.maximum(room, 0))
    moved = jax.random.randint(jax.random.fold_in(own, 4), (count // 2,), 0, 1 << 20) % (room + 1)
    sizes = sizes.at[giver].add(-moved).at[taker].add(moved)
    members = jnp.searchsorted(jnp.cumsum(sizes), jnp.arange(rows * top), side="right").astype(jnp.int32)
    grid = members.reshape(top, rows).T
    grid = grid[jax.random.permutation(jax.random.fold_in(own, 1), rows)]
    turn = jax.random.randint(jax.random.fold_in(own, 2), (rows, 1), 0, top)
    return jnp.take_along_axis(grid, (jnp.arange(top)[None, :] + turn) % top, axis=1)


def shares(number_of, total, reach, slope, full):
    loads = [(1 << 20) // math.isqrt(rank ** slope) + 1 for rank in range(1, number_of + 1)]
    largest = reach if full else min(reach, max(-(-total // number_of), total * loads[0] // sum(loads)))
    least = 1 if total - largest >= number_of - 1 else 0
    holding, rest = [largest] + [least] * (number_of - 1), total - largest - least * (number_of - 1)
    while rest > 0:
        free = [i for i in range(1, number_of) if holding[i] < largest] or [i for i in range(1, number_of) if holding[i] < reach]
        mass, remaining = sum([loads[i] for i in free]), rest
        for i in free:
            addition = min(reach - holding[i], max(1, remaining * loads[i] // mass), rest)
            holding[i] = holding[i] + addition
            rest = rest - addition
    return np.array(holding)


def noise(rng, extent, scale, most, shards=(), kind=jnp.bfloat16):
    result = scale * jax.random.normal(rng, extent, jnp.float32)
    if shards:
        result = result * levels(rng, extent, shards, -0.22, 0.18)
    return jnp.clip(result, -most, most).astype(kind)


def setup_inputs(seed: int = 0) -> dict:
    streams_of = jax.random.split(jax.random.key(seed), 8)
    state = noise(streams_of[0], (NX, NY, NZ, COMP * DOFS), 1.0, 6.0, ((0, 4), (1, 4), (2, 2)), jnp.float32)
    convection = noise(streams_of[1], (NX, NY, NZ, DOFS * DOFS), (4 * DOFS) ** -0.5, 0.375, ((0, 4), (1, 4), (2, 2)))
    inverse_mass = noise(streams_of[2], (NX, NY, NZ, DOFS * DOFS), DOFS ** -0.5, 0.75, ((0, 4), (1, 4), (2, 2)))
    face_coupling = noise(streams_of[3], (96, DOFS), 384 ** -0.5, 0.3125)
    lower_bound = jnp.clip(-3.0 + 2.0 * jax.random.uniform(streams_of[4], (NX, NY, NZ, COMP * DOFS), jnp.float32) ** levels(streams_of[4], (NX, NY, NZ, COMP * DOFS), ((0, 4), (1, 4), (2, 2)), -0.2, 0.2), -3.0, -1.0)
    upper_bound = jnp.clip(1.0 + 2.0 * jax.random.uniform(streams_of[5], (NX, NY, NZ, COMP * DOFS), jnp.float32) ** levels(streams_of[5], (NX, NY, NZ, COMP * DOFS), ((0, 4), (1, 4), (2, 2)), -0.2, 0.2), 1.0, 3.0)
    new_owner_keys = jax.random.split(jax.random.fold_in(streams_of[6], 1), DEVICES * ZONES_DEV // ZONES_DEV)
    new_owner_turns = jax.random.permutation(jax.random.fold_in(streams_of[6], 3), DEVICES * ZONES_DEV // ZONES_DEV)
    new_owner = jax.vmap(lambda own, number: shared_out(jax.random.fold_in(streams_of[6], 2), own, number, ZONES_DEV, DEVICES, 1, CAP, 2))(new_owner_keys, new_owner_turns).reshape((DEVICES, ZONES_DEV, 1))
    return dict(state=state, convection=convection, inverse_mass=inverse_mass, face_coupling=face_coupling, lower_bound=lower_bound, upper_bound=upper_bound, new_owner=new_owner)


HIGH = lax.Precision.HIGHEST


def neighbour(face, axis, lower):
    count = face.shape[axis]
    widths = [(0, 0)] * face.ndim
    if lower:
        widths[axis] = (1, 0)
        return lax.slice_in_dim(jnp.pad(face, widths), 0, count, axis=axis)
    widths[axis] = (0, 1)
    return lax.slice_in_dim(jnp.pad(face, widths), 1, count + 1, axis=axis)


def remap(state, convection, inverse_mass, face_coupling, lower_bound, upper_bound):
    nx, ny, nz = state.shape[0], state.shape[1], state.shape[2]
    work = state.astype(jnp.bfloat16)
    cube = work.reshape(nx, ny, nz, COMP, 4, 4, 4)

    def flat(face):
        return face.reshape(nx, ny, nz, COMP, 16)

    incoming = jnp.concatenate([
        neighbour(flat(cube[:, :, :, :, 3, :, :]), 0, True),
        neighbour(flat(cube[:, :, :, :, 0, :, :]), 0, False),
        neighbour(flat(cube[:, :, :, :, :, 3, :]), 1, True),
        neighbour(flat(cube[:, :, :, :, :, 0, :]), 1, False),
        neighbour(flat(cube[:, :, :, :, :, :, 3]), 2, True),
        neighbour(flat(cube[:, :, :, :, :, :, 0]), 2, False)], axis=-1)
    flux = jnp.einsum("xyzcf,fi->xyzci", incoming.astype(jnp.float32), face_coupling.astype(jnp.float32), precision=HIGH)

    def slab(pieces):
        conv, inverse, worked, flowing, current, lower, upper = pieces
        conv = conv.astype(jnp.float32).reshape(ny, nz, DOFS, DOFS)
        inverse = inverse.astype(jnp.float32).reshape(ny, nz, DOFS, DOFS)
        values = worked.astype(jnp.float32).reshape(ny, nz, COMP, DOFS)
        pushed = jnp.einsum("yzij,yzcj->yzci", conv, values, precision=HIGH)
        rhs = (pushed + flowing).astype(jnp.bfloat16)
        rhs = lax.optimization_barrier(rhs).astype(jnp.float32)
        change = jnp.einsum("yzij,yzcj->yzci", inverse, rhs, precision=HIGH)
        moved = current + change.reshape(ny, nz, COMP * DOFS)
        return jnp.minimum(jnp.maximum(moved, lower), upper)

    return lax.map(slab, (convection, inverse_mass, work, flux, state, lower_bound, upper_bound))


def reference(state, convection, inverse_mass, face_coupling, lower_bound, upper_bound, new_owner):
    for step in range(STEPS):
        state = remap(state, convection, inverse_mass, face_coupling, lower_bound, upper_bound)
    devices = N_GX * N_GY * N_GZ
    width = COMP * DOFS
    blocks = state.reshape(N_GX, EX, N_GY, EY, N_GZ, EZ, width)
    blocks = blocks.transpose(0, 2, 4, 1, 3, 5, 6).reshape(devices, EX * EY * EZ, width)
    owner = new_owner[:, :, 0].astype(jnp.int32)
    onehot = (owner[:, :, None] == jnp.arange(devices, dtype=jnp.int32)[None, None, :]).astype(jnp.int32)
    running = jnp.cumsum(onehot, axis=1).astype(jnp.int32)
    rank = (jnp.sum(running * onehot, axis=2) - 1).astype(jnp.int32)
    slot = (owner * CAP + rank).astype(jnp.int32)

    def place(target, rows):
        return jnp.zeros((devices * CAP, width), rows.dtype).at[target].set(rows)

    sent = jax.vmap(place)(slot, blocks)
    return sent.reshape(devices, devices, CAP, width).transpose(1, 0, 2, 3).reshape(devices * devices * CAP, width)
```

```python
import functools
import jax
import jax.numpy as jnp
from jax import lax
from jax.experimental import pallas as pl
from jax.experimental.pallas import tpu as pltpu
from jax.sharding import PartitionSpec as P

COMP = 4
DOFS = 64
WIDTH = COMP * DOFS
STEPS = 2
LANES = 256
WIDE = (True, True)
MESH = pl.DeviceIdType.MESH
BF = jnp.bfloat16
F32 = jnp.float32
NT = (((1,), (1,)), ((), ()))


def face_tables(face_coupling):
    columns = jnp.arange(WIDTH, dtype=jnp.int32)
    component = columns // DOFS
    local = columns % DOFS
    coords = (local // 16, local // 4 % 4, local % 4)
    rests = (4 * coords[1] + coords[2], 4 * coords[0] + coords[2], 4 * coords[0] + coords[1])
    outputs = jnp.arange(COMP * 16, dtype=jnp.int32)
    picks = []
    couples = []
    identity = jnp.eye(COMP, dtype=BF)
    for direction in range(3):
        for side, level in ((0, 3), (1, 0)):
            match = (
                (coords[direction] == level)[None, :]
                & (component[None, :] == (outputs // 16)[:, None])
                & (rests[direction][None, :] == (outputs % 16)[:, None])
            )
            picks.append(match.astype(BF))
            face = 2 * direction + side
            block = face_coupling[16 * face : 16 * face + 16]
            couples.append(
                (identity[:, None, :, None] * block.T[None, :, None, :]).reshape(WIDTH, COMP * 16)
            )
    return jnp.concatenate(picks, axis=0), jnp.concatenate(couples, axis=1)


def kernel(
    dims, cap,
    state_ref, lower_ref, upper_ref, slot_ref, pick_ref, couple_ref, eye_ref, gather_ref,
    conv_hbm, inv_hbm, out_ref,
    conv_raw, inv_raw, conv_t, inv_t, state_t, lower_t, upper_t, work, rhs, partial,
    faces, landed, load_sem, send_sem, recv_sem,
):
    zones = state_ref.shape[0]
    blocks = zones // LANES
    axes = ("gx", "gy", "gz")
    counts = [lax.axis_size(a) for a in axes]
    place = [lax.axis_index(a) for a in axes]
    strides = (dims[1] * dims[2], dims[2], 1)

    def loads(block, inverse):
        part = pl.ds(block * LANES, LANES)
        if inverse:
            return pltpu.make_async_copy(inv_hbm.at[part], inv_raw.at[part], load_sem.at[blocks + block])
        return pltpu.make_async_copy(conv_hbm.at[part], conv_raw.at[part], load_sem.at[block])

    for block in range(blocks):
        loads(block, False).start()
    for block in range(blocks):
        loads(block, True).start()

    landed[...] = jnp.zeros_like(landed)
    barrier = pltpu.get_barrier_semaphore()
    ups = [place[d] < counts[d] - 1 for d in range(3)]
    downs = [place[d] > 0 for d in range(3)]
    for d in range(3):
        @pl.when(ups[d])
        def _(d=d):
            pl.semaphore_signal(barrier, 1, device_id={axes[d]: place[d] + 1}, device_id_type=MESH)

        @pl.when(downs[d])
        def _(d=d):
            pl.semaphore_signal(barrier, 1, device_id={axes[d]: place[d] - 1}, device_id_type=MESH)
    pl.semaphore_wait(barrier, sum(flag.astype(jnp.int32) for flag in ups + downs))

    for block in range(blocks):
        part = pl.ds(block * LANES, LANES)
        state_t[:, part] = state_ref[part, :].T
        lower_t[:, part] = lower_ref[part, :].T
        upper_t[:, part] = upper_ref[part, :].T

    rows = COMP * 16

    def exchange(step, d, side):
        row = pl.ds((2 * d + side) * rows, rows)
        if d == 0:
            near = zones - strides[0] if side == 0 else 0
            lane = pl.ds(near, strides[0])
        else:
            lane = pl.ds(0, zones)
        return pltpu.make_async_remote_copy(
            src_ref=faces.at[step, row, lane],
            dst_ref=landed.at[step, row, lane],
            send_sem=send_sem.at[step, 2 * d + side],
            recv_sem=recv_sem.at[step, 2 * d + side],
            device_id={axes[d]: place[d] + 1 if side == 0 else place[d] - 1},
            device_id_type=MESH,
        )

    def transposed(raw, target, block):
        @pl.loop(0, DOFS * DOFS // LANES)
        def _(chunk):
            col = pl.ds(pl.multiple_of(chunk * LANES, LANES), LANES)
            part = pl.ds(block * LANES, LANES)
            target[col, part] = lax.dot_general(
                eye_ref[...], raw[part, col], NT, preferred_element_type=F32
            ).astype(BF)

    def apply(matrix, vector, block, wide):
        part = pl.ds(block * LANES, LANES)

        @pl.loop(0, DOFS // 4)
        def _(group):
            for half in range(LANES // 128):
                lane = pl.ds(block * LANES + half * 128, 128)
                small = pl.ds(half * 128, 128)
                vecs = [
                    [vector[c * DOFS + 16 * b : c * DOFS + 16 * b + 16, lane] for b in range(4)]
                    for c in range(COMP)
                ]
                if wide:
                    vecs = [[piece.astype(F32) for piece in v] for v in vecs]
                for i in range(4):
                    base = pl.multiple_of(group * 256 + i * 64, 64)
                    m = [matrix[pl.ds(base + 16 * b, 16), lane] for b in range(4)]
                    if wide:
                        m = [piece.astype(F32) for piece in m]
                    for c in range(COMP):
                        v = vecs[c]
                        total = (m[0] * v[0] + m[1] * v[1]) + (m[2] * v[2] + m[3] * v[3])
                        slot = pl.ds(pl.multiple_of(group * 64 + i * 16, 16), 16)
                        partial[c, slot, small] = total.astype(BF)

        return [
            jnp.dot(gather_ref[...], partial[c], preferred_element_type=F32) for c in range(COMP)
        ]

    lane_id = lax.broadcasted_iota(jnp.int32, (rows, zones), 1)

    for step in range(STEPS):
        work[...] = state_t[...].astype(BF)
        faces[step] = jnp.dot(pick_ref[...], work[...], preferred_element_type=F32).astype(BF)
        for d in range(3):
            @pl.when(ups[d])
            def _(d=d):
                exchange(step, d, 0).start()

            @pl.when(downs[d])
            def _(d=d):
                exchange(step, d, 1).start()
        pushed = []
        for block in range(blocks):
            part = pl.ds(block * LANES, LANES)
            if step == 0:
                loads(block, False).wait()
                transposed(conv_raw, conv_t, block)
            for c, value in enumerate(apply(conv_t, work, block, WIDE[0])):
                rhs[c * DOFS : (c + 1) * DOFS, part] = value
        flux = None
        for d in range(3):
            @pl.when(downs[d])
            def _(d=d):
                exchange(step, d, 0).wait_recv()

            @pl.when(ups[d])
            def _(d=d):
                exchange(step, d, 1).wait_recv()
        for d in range(3):
            s = strides[d]
            n = dims[d]
            index = lane_id // s % n
            far = (n - 1) * s
            for side in range(2):
                row = pl.ds((2 * d + side) * rows, rows)
                mine = faces[step, row, :].astype(F32)
                other = landed[step, row, :].astype(F32)
                if side == 0:
                    inner = pltpu.roll(mine, s, 1)
                    outer = pltpu.roll(other, zones - far, 1)
                    value = jnp.where(index == 0, outer, inner)
                else:
                    inner = pltpu.roll(mine, zones - s, 1)
                    outer = pltpu.roll(other, far, 1)
                    value = jnp.where(index == n - 1, outer, inner)
                term = jnp.dot(
                    couple_ref[:, (2 * d + side) * rows : (2 * d + side + 1) * rows],
                    value.astype(BF),
                    preferred_element_type=F32,
                )
                flux = term if flux is None else flux + term
        work[...] = (rhs[...] + flux).astype(BF)
        for block in range(blocks):
            part = pl.ds(block * LANES, LANES)
            if step == 0:
                loads(block, True).wait()
                transposed(inv_raw, inv_t, block)
            for c, value in enumerate(apply(inv_t, work, block, WIDE[1])):
                row = slice(c * DOFS, (c + 1) * DOFS)
                moved = state_t[row, part] + value
                state_t[row, part] = jnp.minimum(
                    jnp.maximum(moved, lower_t[row, part]), upper_t[row, part]
                )
        for d in range(3):
            @pl.when(ups[d])
            def _(d=d):
                exchange(step, d, 0).wait_send()

            @pl.when(downs[d])
            def _(d=d):
                exchange(step, d, 1).wait_send()

    work[...] = state_t[...].astype(BF)
    slots = jnp.broadcast_to(slot_ref[...], (LANES, zones))
    level = lax.broadcasted_iota(jnp.int32, (LANES, zones), 0)

    @pl.loop(0, out_ref.shape[0] // LANES)
    def _(group):
        start = pl.multiple_of(group * LANES, LANES)
        onehot = jnp.where(slots == level + start, 1.0, 0.0).astype(BF)
        out_ref[pl.ds(start, LANES), :] = lax.dot_general(
            onehot, work[...], NT, preferred_element_type=F32
        ).astype(BF)


def shards(state, convection, inverse_mass, face_coupling, lower_bound, upper_bound, new_owner):
    ex, ey, ez, width = state.shape
    zones = ex * ey * ez
    devices = lax.axis_size(("gx", "gy", "gz"))
    capacity = max(2, 2 * zones // devices)
    pick, couple = face_tables(face_coupling)
    owner = new_owner[0, :, 0]
    onehot = (owner[:, None] == jnp.arange(devices, dtype=jnp.int32)[None, :]).astype(BF)
    positions = jnp.arange(zones, dtype=jnp.int32)
    lower_tri = (positions[:, None] >= positions[None, :]).astype(BF)
    running = jnp.dot(lower_tri, onehot, preferred_element_type=F32)
    rank = jnp.sum(running * onehot.astype(F32), axis=1).astype(jnp.int32) - 1
    slot = (owner * capacity + rank).reshape(1, zones)
    eye = jnp.eye(LANES, dtype=BF)
    gather = (
        jnp.arange(DOFS)[:, None] == (jnp.arange(DOFS * 16) // 16)[None, :]
    ).astype(BF)
    total = devices * capacity
    vmem = pl.BlockSpec(memory_space=pltpu.VMEM)
    hbm = pl.BlockSpec(memory_space=pl.ANY)
    blocks = zones // LANES
    entries = DOFS * DOFS
    outgoing = pl.pallas_call(
        functools.partial(kernel, (ex, ey, ez), capacity),
        out_shape=jax.ShapeDtypeStruct((total, width), BF),
        in_specs=[vmem] * 8 + [hbm] * 2,
        out_specs=vmem,
        scratch_shapes=[
            pltpu.VMEM((zones, entries), BF),
            pltpu.VMEM((zones, entries), BF),
            pltpu.VMEM((entries, zones), BF),
            pltpu.VMEM((entries, zones), BF),
            pltpu.VMEM((width, zones), F32),
            pltpu.VMEM((width, zones), F32),
            pltpu.VMEM((width, zones), F32),
            pltpu.VMEM((width, zones), BF),
            pltpu.VMEM((width, zones), F32),
            pltpu.VMEM((COMP, DOFS * 16, LANES), BF),
            pltpu.VMEM((STEPS, 6 * COMP * 16, zones), BF),
            pltpu.VMEM((STEPS, 6 * COMP * 16, zones), BF),
            pltpu.SemaphoreType.DMA((2 * blocks,)),
            pltpu.SemaphoreType.DMA((STEPS, 6)),
            pltpu.SemaphoreType.DMA((STEPS, 6)),
        ],
        compiler_params=pltpu.CompilerParams(
            collective_id=0, has_side_effects=True, vmem_limit_bytes=60 * 1024 * 1024
        ),
    )(
        state.reshape(zones, width), lower_bound.reshape(zones, width),
        upper_bound.reshape(zones, width), slot, pick, couple, eye, gather,
        convection.reshape(zones, entries), inverse_mass.reshape(zones, entries),
    )
    arrived = lax.all_to_all(
        outgoing.reshape(devices, capacity, width),
        ("gx", "gy", "gz"),
        split_axis=0,
        concat_axis=0,
        tiled=True,
    )
    return arrived.reshape(total, width).astype(F32)


def solution(mesh):
    in_specs = (
        P("gx", "gy", "gz", None),
        P("gx", "gy", "gz", None),
        P("gx", "gy", "gz", None),
        P(),
        P("gx", "gy", "gz", None),
        P("gx", "gy", "gz", None),
        P(("gx", "gy", "gz"), None, None),
    )
    out_specs = P(("gx", "gy", "gz"), None)
    return jax.shard_map(shards, mesh=mesh, in_specs=in_specs, out_specs=out_specs, check_vma=False)
```

```python
import functools
import jax
import jax.numpy as jnp
import numpy as np
from jax import lax
from jax.experimental import pallas as pl
from jax.experimental.pallas import tpu as pltpu
from jax.sharding import PartitionSpec as P

COMP = 4
DOFS = 64
WIDTH = COMP * DOFS
STEPS = 2
LANES = 256
MESH = pl.DeviceIdType.MESH
BF = jnp.bfloat16
F32 = jnp.float32
NT = (((1,), (1,)), ((), ()))


def face_picks():
    local = np.arange(DOFS)
    coords = (local // 16, local // 4 % 4, local % 4)
    rests = (4 * coords[1] + coords[2], 4 * coords[0] + coords[2], 4 * coords[0] + coords[1])
    picks = []
    for direction in range(3):
        for level in (3, 0):
            match = (coords[direction] == level) & (rests[direction] == np.arange(16)[:, None])
            picks.append(np.kron(np.eye(COMP), match))
    return np.concatenate(picks, axis=0)


def kernel(
    dims, cap,
    state_ref, lower_ref, upper_ref, owner_ref, pick_ref, couple_ref,
    conv_hbm, inv_hbm, out_ref,
    conv_raw, inv_raw, conv_t, inv_t, state_t, lower_t, upper_t, work, rhs, vector,
    faces, landed, arriving, load_sem, send_sem, recv_sem,
):
    zones = state_ref.shape[0]
    blocks = zones // LANES
    axes = ("gx", "gy", "gz")
    counts = [lax.axis_size(a) for a in axes]
    place = [lax.axis_index(a) for a in axes]
    strides = (dims[1] * dims[2], dims[2], 1)

    def loads(block, inverse):
        part = pl.ds(block * LANES, LANES)
        if inverse:
            return pltpu.make_async_copy(inv_hbm.at[part], inv_raw.at[part], load_sem.at[blocks + block])
        return pltpu.make_async_copy(conv_hbm.at[part], conv_raw.at[part], load_sem.at[block])

    for block in range(blocks):
        loads(block, False).start()
    for block in range(blocks):
        loads(block, True).start()

    landed[...] = jnp.zeros_like(landed)
    barrier = pltpu.get_barrier_semaphore()
    ups = [place[d] < counts[d] - 1 for d in range(3)]
    downs = [place[d] > 0 for d in range(3)]
    for d in range(3):
        @pl.when(ups[d])
        def _(d=d):
            pl.semaphore_signal(barrier, 1, device_id={axes[d]: place[d] + 1}, device_id_type=MESH)

        @pl.when(downs[d])
        def _(d=d):
            pl.semaphore_signal(barrier, 1, device_id={axes[d]: place[d] - 1}, device_id_type=MESH)
    pl.semaphore_wait(barrier, sum(flag.astype(jnp.int32) for flag in ups + downs))

    for block in range(blocks):
        part = pl.ds(block * LANES, LANES)
        state_t[:, part] = state_ref[part, :].T
        lower_t[:, part] = lower_ref[part, :].T
        upper_t[:, part] = upper_ref[part, :].T

    rows = COMP * 16

    def exchange(step, d, side):
        row = pl.ds((2 * d + side) * rows, rows)
        if d == 0:
            near = zones - strides[0] if side == 0 else 0
            lane = pl.ds(near, strides[0])
        else:
            lane = pl.ds(0, zones)
        return pltpu.make_async_remote_copy(
            src_ref=faces.at[step, row, lane],
            dst_ref=landed.at[step, row, lane],
            send_sem=send_sem.at[step, 2 * d + side],
            recv_sem=recv_sem.at[step, 2 * d + side],
            device_id={axes[d]: place[d] + 1 if side == 0 else place[d] - 1},
            device_id_type=MESH,
        )

    level8 = lax.broadcasted_iota(jnp.int32, (8, 128), 0)

    def merged(a, b, stride):
        odd = level8 // stride % 2 == 1
        return jnp.where(odd, b, a) + pltpu.roll(jnp.where(odd, a, b), 8 - stride, 0)

    def turn(raw, target, lane, chunk):
        col = pl.ds(pl.multiple_of(chunk * 128, 128), 128)
        value = raw[lane, col].T

        def store():
            target[col, lane] = value

        return store

    groups = DOFS // 8

    def apply(matrix, block, raw, finish):
        halves = [pl.ds(block * LANES + half * 128, 128) for half in range(LANES // 128)]
        if raw is not None:
            for lane in halves:
                for pair in range(4):
                    turn(raw, matrix, lane, pair)()

        @pl.loop(0, groups)
        def _(group):
            for lane in halves:
                stack = [[] for _ in range(COMP)]
                for pair in range(4):
                    store = None
                    if raw is not None:
                        store = turn(raw, matrix, lane, jnp.minimum(group + 1, groups - 1) * 4 + pair)
                    base = pl.multiple_of(group * 512 + pair * 128, 128)
                    m = [
                        [matrix[pl.ds(base + 64 * i + 16 * b, 16), lane].astype(F32) for b in range(4)]
                        for i in range(2)
                    ]
                    for c in range(COMP):
                        sums = [None, None]
                        for b in range(4):
                            row = c * DOFS + 16 * b
                            v = vector[row : row + 16, lane]
                            for i in range(2):
                                term = m[i][b] * v
                                sums[i] = term if b == 0 else sums[i] + term
                        node = merged(*[total[:8] + total[8:] for total in sums], 1)
                        stride = 2
                        while len(stack[c]) and stack[c][-1][0] == stride:
                            node = merged(stack[c].pop()[1], node, stride)
                            stride *= 2
                        stack[c].append((stride, node))
                    if store is not None:
                        store()
                for c in range(COMP):
                    row = pl.ds(pl.multiple_of(c * DOFS + group * 8, 8), 8)
                    finish(row, lane, stack[c][0][1])

    lane_id = lax.broadcasted_iota(jnp.int32, (rows, zones), 1)

    def keep(row, lane, value):
        rhs[row, lane] = value

    def advance(row, lane, value):
        moved = state_t[row, lane] + value
        state_t[row, lane] = jnp.minimum(jnp.maximum(moved, lower_t[row, lane]), upper_t[row, lane])

    for step in range(STEPS):
        work[...] = state_t[...].astype(BF)
        vector[...] = work[...].astype(F32)
        faces[step] = jnp.dot(pick_ref[...], work[...], preferred_element_type=F32).astype(BF)
        for d in range(3):
            @pl.when(ups[d])
            def _(d=d):
                exchange(step, d, 0).start()

            @pl.when(downs[d])
            def _(d=d):
                exchange(step, d, 1).start()
        for block in range(blocks):
            if step == 0:
                loads(block, False).wait()
            apply(conv_t, block, conv_raw if step == 0 else None, keep)
        for d in range(3):
            @pl.when(downs[d])
            def _(d=d):
                exchange(step, d, 0).wait_recv()

            @pl.when(ups[d])
            def _(d=d):
                exchange(step, d, 1).wait_recv()
        for d in range(3):
            s = strides[d]
            n = dims[d]
            index = lane_id // s % n
            far = (n - 1) * s
            for side in range(2):
                row = pl.ds((2 * d + side) * rows, rows)
                mine = faces[step, row, :].astype(F32)
                other = landed[step, row, :].astype(F32)
                if side == 0:
                    inner = pltpu.roll(mine, s, 1)
                    outer = pltpu.roll(other, zones - far, 1)
                    value = jnp.where(index == 0, outer, inner)
                else:
                    inner = pltpu.roll(mine, zones - s, 1)
                    outer = pltpu.roll(other, far, 1)
                    value = jnp.where(index == n - 1, outer, inner)
                value = value.astype(BF)
                for c in range(COMP):
                    face = 2 * d + side
                    arriving[c, face * 16 : face * 16 + 16, :] = value[c * 16 : c * 16 + 16]
        for c in range(COMP):
            row = slice(c * DOFS, (c + 1) * DOFS)
            flux = jnp.dot(couple_ref[...], arriving[c], preferred_element_type=F32)
            vector[row, :] = (rhs[row, :] + flux).astype(BF).astype(F32)
        for block in range(blocks):
            if step == 0:
                loads(block, True).wait()
            apply(inv_t, block, inv_raw if step == 0 else None, advance)
        for d in range(3):
            @pl.when(ups[d])
            def _(d=d):
                exchange(step, d, 0).wait_send()

            @pl.when(downs[d])
            def _(d=d):
                exchange(step, d, 1).wait_send()

    work[...] = state_t[...].astype(BF)
    owner = owner_ref[...]
    devices = out_ref.shape[0] // cap
    named = lax.broadcasted_iota(jnp.int32, (devices, zones), 0) == owner
    earlier = lax.broadcasted_iota(jnp.int32, (zones, zones), 0) < lax.broadcasted_iota(
        jnp.int32, (zones, zones), 1
    )
    before = jnp.dot(
        jnp.where(named, 1.0, 0.0).astype(BF),
        jnp.where(earlier, 1.0, 0.0).astype(BF),
        preferred_element_type=F32,
    )
    rank = jnp.sum(jnp.where(named, before, 0.0), axis=0, keepdims=True).astype(jnp.int32)
    slots = jnp.broadcast_to(owner * cap + rank, (LANES, zones))
    level = lax.broadcasted_iota(jnp.int32, (LANES, zones), 0)

    @pl.loop(0, out_ref.shape[0] // LANES)
    def _(group):
        start = pl.multiple_of(group * LANES, LANES)
        onehot = jnp.where(slots == level + start, 1.0, 0.0).astype(BF)
        out_ref[pl.ds(start, LANES), :] = lax.dot_general(
            onehot, work[...], NT, preferred_element_type=F32
        ).astype(BF)


def shards(state, convection, inverse_mass, face_coupling, lower_bound, upper_bound, new_owner):
    ex, ey, ez, width = state.shape
    zones = ex * ey * ez
    devices = lax.axis_size(("gx", "gy", "gz"))
    capacity = max(2, 2 * zones // devices)
    pick = jnp.asarray(face_picks(), BF)
    total = devices * capacity
    vmem = pl.BlockSpec(memory_space=pltpu.VMEM)
    hbm = pl.BlockSpec(memory_space=pl.ANY)
    blocks = zones // LANES
    entries = DOFS * DOFS
    outgoing = pl.pallas_call(
        functools.partial(kernel, (ex, ey, ez), capacity),
        out_shape=jax.ShapeDtypeStruct((total, width), BF),
        in_specs=[vmem] * 6 + [hbm] * 2,
        out_specs=vmem,
        scratch_shapes=[
            pltpu.VMEM((zones, entries), BF),
            pltpu.VMEM((zones, entries), BF),
            pltpu.VMEM((entries, zones), BF),
            pltpu.VMEM((entries, zones), BF),
            pltpu.VMEM((width, zones), F32),
            pltpu.VMEM((width, zones), F32),
            pltpu.VMEM((width, zones), F32),
            pltpu.VMEM((width, zones), BF),
            pltpu.VMEM((width, zones), F32),
            pltpu.VMEM((width, zones), F32),
            pltpu.VMEM((STEPS, 6 * COMP * 16, zones), BF),
            pltpu.VMEM((STEPS, 6 * COMP * 16, zones), BF),
            pltpu.VMEM((COMP, 96, zones), BF),
            pltpu.SemaphoreType.DMA((2 * blocks,)),
            pltpu.SemaphoreType.DMA((STEPS, 6)),
            pltpu.SemaphoreType.DMA((STEPS, 6)),
        ],
        compiler_params=pltpu.CompilerParams(
            collective_id=0, has_side_effects=True, vmem_limit_bytes=60 * 1024 * 1024
        ),
    )(
        state.reshape(zones, width), lower_bound.reshape(zones, width),
        upper_bound.reshape(zones, width), new_owner.reshape(1, zones), pick, face_coupling.T,
        convection.reshape(zones, entries), inverse_mass.reshape(zones, entries),
    )
    arrived = lax.all_to_all(
        outgoing.reshape(devices, capacity, width),
        ("gx", "gy", "gz"),
        split_axis=0,
        concat_axis=0,
        tiled=True,
    )
    return arrived.reshape(total, width).astype(F32)


def solution(mesh):
    in_specs = (
        P("gx", "gy", "gz", None),
        P("gx", "gy", "gz", None),
        P("gx", "gy", "gz", None),
        P(),
        P("gx", "gy", "gz", None),
        P("gx", "gy", "gz", None),
        P(("gx", "gy", "gz"), None, None),
    )
    out_specs = P(("gx", "gy", "gz"), None)
    return jax.shard_map(shards, mesh=mesh, in_specs=in_specs, out_specs=out_specs, check_vma=False)
```
